128 devices in a mesh: pair: 16 (over x_lo, y, core), win: 8 (over x_hi, z).
Axes of the slice: x: 4 (x_hi: 2, x_lo: 2; x = x_hi * 2 + x_lo), y: 4, z: 4, core: 2. Of those that a mesh axis runs over, the one named last changes fastest.
Arguments:
- traces: bfloat16 [4096, 256, 1024], P('pair', 'win'), may hold values from -210 to 210, as said below
- partner: int32 [2, 16], replicated, may hold values from 0 to 15, as said below
- block_ids: int32 [16], replicated, may hold values from 0 to 15, each once
Outputs:
- correlations: float32 [2, 32, 2, 4096, 256], P(None, 'win', None, 'pair')
The draws below stay inside these ranges and needn't reach their ends.
Inputs may be any that keep to these rules, and one draw needn't show every extreme that they name: traces are noise whose amplitude and spectral colour vary from channel to channel and window to window. Each row of partner pairs every fibre block with one other block: partner[r, partner[r, b]] = b and partner[r, b] != b; the rows are distinct rounds of one round-robin plan. block_ids names each fibre block once.
All inputs are finite; a program needn't handle non-finite values.
Results may differ from the reference program's by a relative error of at most 0.0058.
Values may be sent and summed in bfloat16 or wider, within the bound.
A program may use at most 128 MiB of HBM per device.

```python
import math
import jax
import jax.numpy as jnp
from jax import lax

BLK = 256
SAMPLES = 1024
BINS = 32
FIRST_BIN = 16
BIN_STEP = 8
ROUNDS = 2
CHANNELS = 4096
WINDOWS = 256
N_PAIR = 16


def draw_traces(key, part):
    keys = jax.random.split(key, 5)
    full_shape = (CHANNELS, WINDOWS, SAMPLES + 2)
    base = jnp.clip(jax.random.normal(keys[0], full_shape, jnp.float32), -5.0, 5.0)
    spread = math.log(10.0)
    first_tap = jax.random.uniform(keys[2], (CHANNELS, WINDOWS, 1), jnp.float32, -0.9, 0.9)
    second_tap = jax.random.uniform(keys[3], (CHANNELS, WINDOWS, 1), jnp.float32, -0.6, 0.6)
    coloured = base[:, :, 2:] + first_tap * base[:, :, 1:-1] + second_tap * base[:, :, :-2]
    amplitude = jnp.exp(jax.random.uniform(keys[4], (CHANNELS, WINDOWS, 1), jnp.float32, 0.0, spread))
    return (amplitude * coloured).astype(jnp.bfloat16)


def draw_partner(key, part):
    players = N_PAIR
    odd_count = N_PAIR - 1
    key_rounds, key_label = jax.random.split(key)
    chosen = jax.random.permutation(key_rounds, odd_count)[:ROUNDS].astype(jnp.int32)
    tag_name = jax.random.permutation(key_label, players).astype(jnp.int32)
    seats = jnp.arange(players, dtype=jnp.int32)
    others = (2 * chosen[:, None] - seats[None, :]) % odd_count
    anchor_pairing = jnp.where(seats[None, :] == chosen[:, None], odd_count, others)
    anchor_pairing = jnp.where(seats[None, :] == odd_count, chosen[:, None], anchor_pairing)
    renamed_tags = tag_name[anchor_pairing]
    final_output = jnp.zeros((ROUNDS, players), jnp.int32)
    pairing_round_rows = jnp.broadcast_to(jnp.arange(ROUNDS, dtype=jnp.int32)[:, None], (ROUNDS, players))
    column_numbers = jnp.broadcast_to(tag_name[None, :], (ROUNDS, players))
    return final_output.at[pairing_round_rows, column_numbers].set(renamed_tags)


def setup_inputs(seed: int = 0) -> dict:
    key_of = jax.random.split(jax.random.key(seed), 4)
    return {
        "traces": draw_traces(jax.random.fold_in(key_of[3], 71), 0),
        "partner": draw_partner(jax.random.fold_in(key_of[3], 71), 0),
        "block_ids": jax.random.permutation(key_of[2], N_PAIR).astype(jnp.int32),
    }


def tapered_table():
    sample = jnp.arange(SAMPLES, dtype=jnp.int32)
    freq = FIRST_BIN + BIN_STEP * jnp.arange(BINS, dtype=jnp.int32)
    phase = sample[:, None] * freq[None, :] % SAMPLES
    angle = 2.0 * math.pi / SAMPLES * phase.astype(jnp.float32)
    taper = 0.5 - 0.5 * jnp.cos(2.0 * math.pi / SAMPLES * sample.astype(jnp.float32))
    real_part = taper[:, None] * jnp.cos(angle)
    imag_part = -taper[:, None] * jnp.sin(angle)
    return jnp.concatenate([real_part, imag_part], axis=1).astype(jnp.bfloat16)

def whitened(trace_rows, dft_table):
    raw = jnp.dot(trace_rows, dft_table, preferred_element_type=jnp.float32)
    power = lax.optimization_barrier(jnp.mean(raw * raw, axis=-1, keepdims=True))
    return (raw * lax.rsqrt(power + 1e-05)).astype(jnp.bfloat16)

def reference(traces, partner, block_ids):
    dft_table = tapered_table()
    blocks = traces.reshape(N_PAIR, BLK * WINDOWS, SAMPLES)
    spectra = lax.map(lambda trace_rows: whitened(trace_rows, dft_table), blocks)
    spectra = spectra.reshape(N_PAIR, BLK, WINDOWS, 2, BINS).transpose(0, 3, 4, 2, 1)
    holder = jnp.argsort(block_ids).astype(jnp.int32)
    local_spec = spectra.astype(jnp.float32)
    rotated = jnp.concatenate([local_spec[:, 1:2], -local_spec[:, 0:1]], axis=1)
    stacked = jnp.stack([local_spec, rotated], axis=1)
    stack_scale = 1.0 / math.sqrt(WINDOWS)
    results = []
    for round_no in range(ROUNDS):
        partner_dev = holder[partner[round_no][block_ids]].astype(jnp.int32)
        remote = spectra[partner_dev].astype(jnp.float32)
        corr = jnp.einsum('nkcbwi,ncbwj->bknij', stacked, remote, precision=lax.Precision.HIGHEST)
        corr = corr * stack_scale
        results.append(corr.reshape(BINS, 2, CHANNELS, BLK))
    return jnp.stack(results, axis=0)
```

```python
import functools
import math

import jax
import jax.numpy as jnp
import numpy as np
from jax import lax
from jax.experimental import pallas as pl
from jax.experimental.pallas import tpu as pltpu
from jax.sharding import PartitionSpec as P

SAMPLES = 1024
BINS = 32
FIRST_BIN = 16
BIN_STEP = 8
ROUNDS = 2
NY = 4
NZ = 4
N_WIN = 2 * NZ
N_COL = NY * 2
BINS_DEV = BINS // N_WIN
PARTS = 2 * BINS_DEV
WCH = 16
CCH = 128
MESH = pl.DeviceIdType.MESH


def dft_columns():
    sample = np.arange(SAMPLES)
    freq = FIRST_BIN + BIN_STEP * np.arange(BINS)
    angle = 2.0 * np.pi / SAMPLES * (sample[:, None] * freq[None, :] % SAMPLES)
    taper = 0.5 - 0.5 * np.cos(2.0 * np.pi / SAMPLES * sample)
    both = np.stack([taper[:, None] * np.cos(angle), -taper[:, None] * np.sin(angle)], axis=2)
    return jnp.asarray(both.reshape(SAMPLES, 2 * BINS).astype(np.float32), dtype=jnp.bfloat16)


def spread_kernel(
    x_hbm, table, partner, block_ids, lhs_out, rem_out,
    raw, ybuf, lhs, targets,
    xsem, s1, r1, s2, r2, s3, r3, s4, r4, l4, lsem, *buffers,
):
    pair = lax.axis_index("pair")
    win = lax.axis_index("win")
    xlo, col = pair // N_COL, pair % N_COL
    y, core = col // 2, col % 2
    xhi, z = win // NZ, win % NZ
    chunks = len(buffers) // 5
    xbufs, sends, owns, mids, sbufs = (buffers[i * chunks : (i + 1) * chunks] for i in range(5))
    halves = lhs.shape[3] // (2 * N_WIN * WCH)

    def x_copy(g):
        h, v = g // halves, g % halves
        return pltpu.make_async_copy(
            x_hbm.at[pl.ds(h * CCH, CCH), pl.ds(v * WCH, WCH)], xbufs[g], xsem.at[g]
        )

    for g in range(chunks):
        x_copy(g).start()

    win_peers = [((xhi + a) % 2) * NZ + (z + b) % NZ for a in range(2) for b in range(NZ)][1:]
    col_peers = [((y + a) % NY) * 2 + (core + b) % 2 for a in range(NY) for b in range(2)][1:]
    mirror = ((1 - xlo) * N_COL + col, win)

    barrier = pltpu.get_barrier_semaphore()
    for peer in win_peers:
        pl.semaphore_signal(barrier, inc=1, device_id=(pair, peer), device_id_type=MESH)
    for peer in col_peers:
        pl.semaphore_signal(barrier, inc=1, device_id=(xlo * N_COL + peer, win), device_id_type=MESH)
    pl.semaphore_signal(barrier, inc=1, device_id=mirror, device_id_type=MESH)

    @pl.loop(0, ROUNDS)
    def _(r):
        @pl.loop(0, N_COL)
        def _(d):
            wanted = partner[r, block_ids[xlo * N_COL + d]]

            def look(q, found):
                return jnp.where(block_ids[q] == wanted, q, found)

            targets[r, d] = lax.fori_loop(0, 2 * N_COL, look, jnp.int32(0))

    def remote(src, dst, send, recv, device):
        return pltpu.make_async_remote_copy(
            src_ref=src, dst_ref=dst, send_sem=send, recv_sem=recv, device_id=device, device_id_type=MESH
        )

    def transform(g):
        x_copy(g).wait()
        rows = min(512, CCH * WCH)

        @pl.loop(0, CCH * WCH // rows)
        def _(i):
            block = xbufs[g][pl.ds(i * (rows // WCH), rows // WCH)].reshape(rows, SAMPLES)
            raw[pl.ds(i * rows, rows), :] = jnp.dot(block, table[...], preferred_element_type=jnp.float32)

        @pl.loop(0, WCH)
        def _(w):
            part = raw[pl.ds(w, CCH, stride=WCH), :].T[: 2 * BINS]
            power = jnp.sum(part * part, axis=0, keepdims=True) * (1.0 / (2 * BINS))
            ybuf[pl.ds(w, 2 * BINS, stride=WCH), :] = part * lax.rsqrt(power + 1e-05)

        sends[g][...] = ybuf[...].astype(jnp.bfloat16).reshape(N_WIN, PARTS, WCH, CCH)

    def phase1(g):
        for peer in win_peers:
            remote(sends[g].at[peer], owns[g].at[win], s1.at[g], r1.at[g, win], (pair, peer)).start()
        owns[g][win] = sends[g][win]

    def phase2(g):
        for peer in win_peers:
            remote(sends[g].at[peer], owns[g].at[peer], s1.at[g], r1.at[g, peer], (pair, peer)).wait_recv()
        for peer in col_peers:
            remote(
                owns[g].at[peer], mids[g].at[pair], s2.at[g], r2.at[g, col], (xlo * N_COL + peer, win)
            ).start()
        mids[g][pair] = owns[g][col]

    def phase3(g):
        remote(mids[g].at[pair], mids[g].at[pair], s3.at[g], r3.at[g], mirror).start()
        for peer in col_peers:
            slot = xlo * N_COL + peer
            remote(owns[g].at[peer], mids[g].at[slot], s2.at[g], r2.at[g, peer], (slot, win)).wait_recv()
            remote(mids[g].at[slot], mids[g].at[slot], s3.at[g], r3.at[g], mirror).start()

    def phase4(g):
        theirs = mids[g].at[pl.ds((1 - xlo) * N_COL, N_COL)]
        remote(theirs, theirs, s3.at[g], r3.at[g], mirror).wait_recv()
        for peer in [*col_peers, col]:
            for r in range(ROUNDS):
                sbufs[g][peer, r] = mids[g][targets[r, peer]]
            if peer is col:
                pltpu.make_async_copy(sbufs[g].at[col], rem_out.at[g, col], l4.at[g]).start()
            else:
                remote(
                    sbufs[g].at[peer], rem_out.at[g, col], s4.at[g], r4.at[g], (xlo * N_COL + peer, win)
                ).start()

    def left_side(g):
        h, v = g // halves, g % halves
        rows = pl.ds(h * CCH, CCH)
        span = N_WIN * WCH
        for k in range(BINS_DEV):
            for c in range(2):
                part = owns[g][:, 2 * k + c].reshape(span, CCH).astype(jnp.float32).T
                plain = part.astype(jnp.bfloat16)
                turned = (part if c else -part).astype(jnp.bfloat16)
                lhs[k, 0, rows, pl.ds((c * halves + v) * span, span)] = plain
                lhs[k, 1, rows, pl.ds(((1 - c) * halves + v) * span, span)] = turned

    transform(0)
    pl.semaphore_wait(barrier, len(win_peers) + len(col_peers) + 1)
    phase1(0)
    transform(1)
    phase1(1)
    phase2(0)
    transform(2)
    phase1(2)
    phase3(0)
    phase2(1)
    transform(3)
    phase1(3)
    phase4(0)
    phase3(1)
    phase2(2)
    left_side(0)
    phase2(3)
    left_side(1)
    phase4(1)
    phase3(2)
    left_side(2)
    phase3(3)
    left_side(3)
    lhs_copy = pltpu.make_async_copy(lhs, lhs_out, lsem)
    lhs_copy.start()
    phase4(2)
    phase4(3)

    lhs_copy.wait()
    for g in range(chunks):
        seven = owns[g].at[pl.ds(0, N_WIN - 1)]
        eight = mids[g].at[pl.ds(0, N_COL)]
        rounds = sbufs[g].at[pl.ds(0, N_COL - 1)]
        landed = rem_out.at[g, pl.ds(0, N_COL - 1)]
        remote(seven, seven, s1.at[g], r1.at[g, 0], mirror).wait_send()
        remote(seven, seven, s2.at[g], r2.at[g, 0], mirror).wait_send()
        remote(eight, eight, s3.at[g], r3.at[g], mirror).wait_send()
        remote(rounds, landed, s4.at[g], r4.at[g], mirror).wait_send()
        pltpu.make_async_copy(sbufs[g].at[col], rem_out.at[g, col], l4.at[g]).wait()
        remote(rounds, landed, s4.at[g], r4.at[g], mirror).wait_recv()


def spread(traces, partner, block_ids):
    channels, windows, _ = traces.shape
    chans, halves = channels // CCH, windows // WCH
    chunks = chans * halves
    piece = (PARTS, WCH, CCH)
    bf16 = jnp.bfloat16
    lhs_shape = (BINS_DEV, 2, channels, 2 * N_WIN * windows)
    rem_shape = (chunks, N_COL, ROUNDS, *piece)
    dma = pltpu.SemaphoreType.DMA
    table = jnp.pad(dft_columns(), ((0, 0), (0, 128 - 2 * BINS)))
    return pl.pallas_call(
        spread_kernel,
        out_shape=(jax.ShapeDtypeStruct(lhs_shape, bf16), jax.ShapeDtypeStruct(rem_shape, bf16)),
        in_specs=[
            pl.BlockSpec(memory_space=pl.ANY),
            pl.BlockSpec(memory_space=pltpu.VMEM),
            pl.BlockSpec(memory_space=pltpu.SMEM),
            pl.BlockSpec(memory_space=pltpu.SMEM),
        ],
        out_specs=(pl.BlockSpec(memory_space=pl.ANY), pl.BlockSpec(memory_space=pl.ANY)),
        scratch_shapes=[
            pltpu.VMEM((CCH * WCH, 128), jnp.float32),
            pltpu.VMEM((2 * BINS * WCH, CCH), jnp.float32),
            pltpu.VMEM(lhs_shape, bf16),
            pltpu.SMEM((ROUNDS, N_COL), jnp.int32),
            dma((chunks,)),
            dma((chunks,)), dma((chunks, N_WIN)),
            dma((chunks,)), dma((chunks, N_COL)),
            dma((chunks,)), dma((chunks,)),
            dma((chunks,)), dma((chunks,)),
            dma((chunks,)),
            dma,
            *[pltpu.VMEM((CCH, WCH, SAMPLES), bf16)] * chunks,
            *[pltpu.VMEM((N_WIN, *piece), bf16)] * (2 * chunks),
            *[pltpu.VMEM((2 * N_COL, *piece), bf16)] * chunks,
            *[pltpu.VMEM((N_COL, ROUNDS, *piece), bf16)] * chunks,
        ],
        compiler_params=pltpu.CompilerParams(
            collective_id=0, has_side_effects=True, vmem_limit_bytes=50 * 1024 * 1024
        ),
        name="spread",
    )(traces, table, partner, block_ids)


def correlate_kernel(scale, lhs, rem, out):
    chunks, n_win = rem.shape[:2]
    channels = lhs.shape[2]
    chans = channels // CCH
    halves = chunks // chans
    columns = []
    for h in range(chans):
        rows = [
            rem[h * halves + v, :, 0, c].reshape(n_win * WCH, CCH) for c in range(2) for v in range(halves)
        ]
        columns.append(jnp.concatenate(rows, axis=0))
    right = jnp.concatenate(columns, axis=1)
    left = lhs[0].reshape(2 * channels, lhs.shape[3])
    result = jnp.dot(left, right, preferred_element_type=jnp.float32) * scale
    out[0, 0] = result.reshape(out.shape[2:])


def correlate(lhs, rem, scale):
    chunks, n_win = rem.shape[:2]
    bins, _, channels, depth = lhs.shape
    out_shape = (ROUNDS, bins, 2, channels, channels)
    return pl.pallas_call(
        functools.partial(correlate_kernel, scale),
        grid=(bins, ROUNDS),
        out_shape=jax.ShapeDtypeStruct(out_shape, jnp.float32),
        in_specs=[
            pl.BlockSpec((1, 2, channels, depth), lambda k, r: (k, 0, 0, 0)),
            pl.BlockSpec((chunks, n_win, 1, 2, WCH, CCH), lambda k, r: (0, 0, r, k, 0, 0)),
        ],
        out_specs=pl.BlockSpec((1, 1, 2, channels, channels), lambda k, r: (r, k, 0, 0, 0)),
        name="correlate",
    )(lhs, rem)


def local(traces, partner, block_ids):
    windows = traces.shape[1] * N_WIN
    lhs, rem = spread(traces, partner, block_ids)
    return correlate(lhs, rem, 1.0 / math.sqrt(windows))


def solution(mesh):
    placed = (P("pair", "win", None), P(), P())
    return jax.shard_map(
        local,
        mesh=mesh,
        in_specs=placed,
        out_specs=P(None, "win", None, "pair", None),
        check_vma=False,
    )
```

```python
import functools
import math

import jax
import jax.numpy as jnp
import numpy as np
from jax import lax
from jax.experimental import pallas as pl
from jax.experimental.pallas import tpu as pltpu
from jax.sharding import PartitionSpec as P

SAMPLES = 1024
BINS = 32
FIRST_BIN = 16
BIN_STEP = 8
ROUNDS = 2
NY = 4
NZ = 4
N_WIN = 2 * NZ
N_COL = NY * 2
BINS_DEV = BINS // N_WIN
PARTS = 2 * BINS_DEV
WCH = 8
JOIN = 2
LAGS = (2, 4, 6)
CCH = 128
MESH = pl.DeviceIdType.MESH


def dft_columns():
    sample = np.arange(SAMPLES)
    freq = FIRST_BIN + BIN_STEP * np.arange(BINS)
    angle = 2.0 * np.pi / SAMPLES * (sample[:, None] * freq[None, :] % SAMPLES)
    taper = 0.5 - 0.5 * np.cos(2.0 * np.pi / SAMPLES * sample)
    both = np.stack([taper[:, None] * np.cos(angle), -taper[:, None] * np.sin(angle)], axis=2)
    return jnp.asarray(both.reshape(SAMPLES, 2 * BINS).astype(np.float32), dtype=jnp.bfloat16)


def spread_kernel(
    x_hbm, table_hbm, partner_hbm, ids_hbm, lhs_out, rem_out,
    table, partner, block_ids, raw0, raw1, ybuf, lhs, targets,
    xsem, tsem, s1, r1, s2, r2, s3, r3, s4, r4, l4, lsem, *buffers,
):
    pair = lax.axis_index("pair")
    win = lax.axis_index("win")
    xlo, col = pair // N_COL, pair % N_COL
    y, core = col // 2, col % 2
    xhi, z = win // NZ, win % NZ
    chunks = len(buffers) // 5
    xbufs, sends, owns, mids, sbufs = (buffers[i * chunks : (i + 1) * chunks] for i in range(5))
    raws = (raw0, raw1)
    parts_v = lhs.shape[3] // (2 * N_WIN * WCH)

    win_peers = [((xhi + a) % 2) * NZ + (z + b) % NZ for a in range(2) for b in range(NZ)][1:]
    col_peers = [((y + a) % NY) * 2 + (core + b) % 2 for a in range(NY) for b in range(2)][1:]
    mirror = ((1 - xlo) * N_COL + col, win)

    def x_copy(g):
        h, v = g // parts_v, g % parts_v
        return pltpu.make_async_copy(
            x_hbm.at[pl.ds(h * CCH, CCH), pl.ds(v * WCH, WCH)], xbufs[g], xsem.at[g]
        )

    table_copy = pltpu.make_async_copy(table_hbm, table, tsem.at[0])
    partner_copy = pltpu.make_async_copy(partner_hbm, partner, tsem.at[1])
    ids_copy = pltpu.make_async_copy(ids_hbm, block_ids, tsem.at[2])
    table_copy.start()
    for g in range(chunks):
        x_copy(g).start()
    partner_copy.start()
    ids_copy.start()

    barrier = pltpu.get_barrier_semaphore()
    for peer in win_peers:
        pl.semaphore_signal(barrier, inc=1, device_id=(pair, peer), device_id_type=MESH)
    for peer in col_peers:
        pl.semaphore_signal(barrier, inc=1, device_id=(xlo * N_COL + peer, win), device_id_type=MESH)
    pl.semaphore_signal(barrier, inc=1, device_id=mirror, device_id_type=MESH)

    def find_targets():
        partner_copy.wait()
        ids_copy.wait()

        @pl.loop(0, ROUNDS)
        def _(r):
            @pl.loop(0, N_COL)
            def _(d):
                wanted = partner[r, block_ids[xlo * N_COL + d]]
                found = jnp.int32(0)
                for q in range(2 * N_COL):
                    found = jnp.where(block_ids[q] == wanted, q, found)
                targets[r, d] = found

    def remote(src, dst, send, recv, device):
        return pltpu.make_async_remote_copy(
            src_ref=src, dst_ref=dst, send_sem=send, recv_sem=recv, device_id=device, device_id_type=MESH
        )

    blocks = 4
    rows = CCH * WCH // blocks

    def product(g, i):
        block = xbufs[g][pl.ds(i * (rows // WCH), rows // WCH)].reshape(rows, SAMPLES)
        raws[g % 2][pl.ds(i * rows, rows), :] = jnp.dot(block, table[...], preferred_element_type=jnp.float32)

    def whiten(g, w):
        part = raws[g % 2][pl.ds(w, CCH, stride=WCH), :].T[: 2 * BINS]
        power = jnp.sum(part * part, axis=0, keepdims=True) * (1.0 / (2 * BINS))
        ybuf[pl.ds(w, 2 * BINS, stride=WCH), :] = part * lax.rsqrt(power + 1e-05)

    def load(g):
        x_copy(g).wait()

    def product_all(g):
        load(g)

        @pl.loop(0, blocks)
        def _(i):
            product(g, i)

    def whiten_all(g):
        for w in range(WCH):
            whiten(g, w)

    def both(g):
        load(g + 1)

        @pl.loop(0, blocks)
        def _(i):
            product(g + 1, i)
            for w in range(WCH // blocks):
                whiten(g, i * (WCH // blocks) + w)

    def transform(g):
        if g == 0:
            table_copy.wait()
            product_all(0)
            whiten_all(0)
        elif g == chunks - 1:
            whiten_all(g)
        else:
            if g == 1:
                product_all(1)
            both(g)
        sends[g][...] = ybuf[...].astype(jnp.bfloat16).reshape(N_WIN, PARTS, WCH, CCH)

    def phase1(g):
        for peer in win_peers:
            remote(sends[g].at[peer], owns[g].at[win], s1.at[g], r1.at[g, win], (pair, peer)).start()
        owns[g][win] = sends[g][win]

    def phase2(g):
        for peer in win_peers:
            remote(sends[g].at[peer], owns[g].at[peer], s1.at[g], r1.at[g, peer], (pair, peer)).wait_recv()
        for peer in col_peers:
            remote(
                owns[g].at[peer], mids[g].at[pair], s2.at[g], r2.at[g, col], (xlo * N_COL + peer, win)
            ).start()
        mids[g][pair] = owns[g][col]

    def phase3(g):
        remote(mids[g].at[pair], mids[g].at[pair], s3.at[g], r3.at[g], mirror).start()
        for peer in col_peers:
            slot = xlo * N_COL + peer
            remote(owns[g].at[peer], mids[g].at[slot], s2.at[g], r2.at[g, peer], (slot, win)).wait_recv()
            remote(mids[g].at[slot], mids[g].at[slot], s3.at[g], r3.at[g], mirror).start()

    def phase4(g):
        theirs = mids[g].at[pl.ds((1 - xlo) * N_COL, N_COL)]
        remote(theirs, theirs, s3.at[g], r3.at[g], mirror).wait_recv()
        for peer in [*col_peers, col]:
            for r in range(ROUNDS):
                sbufs[g][peer, r] = mids[g][targets[r, peer]]
            if peer is col:
                pltpu.make_async_copy(sbufs[g].at[col], rem_out.at[g, col], l4.at[g]).start()
            else:
                remote(
                    sbufs[g].at[peer], rem_out.at[g, col], s4.at[g], r4.at[g], (xlo * N_COL + peer, win)
                ).start()

    def left_side(g):
        h, v = g // parts_v, g % parts_v
        to = pl.ds(h * CCH, CCH)
        span = N_WIN * WCH
        for k in range(BINS_DEV):
            for c in range(2):
                part = jnp.concatenate(
                    [owns[g + j][:, 2 * k + c].reshape(span, CCH).astype(jnp.float32) for j in range(JOIN)], axis=0
                ).T
                plain = part.astype(jnp.bfloat16)
                turned = (part if c else -part).astype(jnp.bfloat16)
                lhs[k, 0, to, pl.ds((c * parts_v + v) * span, JOIN * span)] = plain
                lhs[k, 1, to, pl.ds(((1 - c) * parts_v + v) * span, JOIN * span)] = turned

    lag2, lag3, lag4 = LAGS
    lhs_copy = pltpu.make_async_copy(lhs, lhs_out, lsem)
    for t in range(chunks + lag4):
        if t < chunks:
            transform(t)
            if t == 0:
                pl.semaphore_wait(barrier, len(win_peers) + len(col_peers) + 1)
            phase1(t)
            if t == 0:
                find_targets()
        if 0 <= t - lag2 < chunks:
            phase2(t - lag2)
        if 0 <= t - lag3 < chunks:
            phase3(t - lag3)
        g = t - lag3 - JOIN + 1
        if 0 <= g < chunks and g % JOIN == 0:
            left_side(g)
            if g == chunks - JOIN:
                lhs_copy.start()
        if 0 <= t - lag4 < chunks:
            phase4(t - lag4)

    lhs_copy.wait()
    for g in range(chunks):
        seven = owns[g].at[pl.ds(0, N_WIN - 1)]
        eight = mids[g].at[pl.ds(0, N_COL)]
        rounds = sbufs[g].at[pl.ds(0, N_COL - 1)]
        landed = rem_out.at[g, pl.ds(0, N_COL - 1)]
        remote(seven, seven, s1.at[g], r1.at[g, 0], mirror).wait_send()
        remote(seven, seven, s2.at[g], r2.at[g, 0], mirror).wait_send()
        remote(eight, eight, s3.at[g], r3.at[g], mirror).wait_send()
        remote(rounds, landed, s4.at[g], r4.at[g], mirror).wait_send()
        pltpu.make_async_copy(sbufs[g].at[col], rem_out.at[g, col], l4.at[g]).wait()
        remote(rounds, landed, s4.at[g], r4.at[g], mirror).wait_recv()


def spread(traces, partner, block_ids):
    channels, windows, _ = traces.shape
    chunks = (channels // CCH) * (windows // WCH)
    piece = (PARTS, WCH, CCH)
    bf16, f32 = jnp.bfloat16, jnp.float32
    lhs_shape = (BINS_DEV, 2, channels, 2 * N_WIN * windows)
    rem_shape = (chunks, N_COL, ROUNDS, *piece)
    dma = pltpu.SemaphoreType.DMA
    table = jnp.pad(dft_columns(), ((0, 0), (0, 128 - 2 * BINS)))
    return pl.pallas_call(
        spread_kernel,
        out_shape=(jax.ShapeDtypeStruct(lhs_shape, bf16), jax.ShapeDtypeStruct(rem_shape, bf16)),
        in_specs=[pl.BlockSpec(memory_space=pltpu.HBM)] * 4,
        out_specs=(pl.BlockSpec(memory_space=pl.ANY), pl.BlockSpec(memory_space=pl.ANY)),
        scratch_shapes=[
            pltpu.VMEM(table.shape, bf16),
            pltpu.SMEM(partner.shape, jnp.int32),
            pltpu.SMEM(block_ids.shape, jnp.int32),
            pltpu.VMEM((CCH * WCH, 128), f32),
            pltpu.VMEM((CCH * WCH, 128), f32),
            pltpu.VMEM((2 * BINS * WCH, CCH), f32),
            pltpu.VMEM(lhs_shape, bf16),
            pltpu.SMEM((ROUNDS, N_COL), jnp.int32),
            dma((chunks,)), dma((3,)),
            dma((chunks,)), dma((chunks, N_WIN)),
            dma((chunks,)), dma((chunks, N_COL)),
            dma((chunks,)), dma((chunks,)),
            dma((chunks,)), dma((chunks,)),
            dma((chunks,)),
            dma,
            *[pltpu.VMEM((CCH, WCH, SAMPLES), bf16)] * chunks,
            *[pltpu.VMEM((N_WIN, *piece), bf16)] * (2 * chunks),
            *[pltpu.VMEM((2 * N_COL, *piece), bf16)] * chunks,
            *[pltpu.VMEM((N_COL, ROUNDS, *piece), bf16)] * chunks,
        ],
        compiler_params=pltpu.CompilerParams(
            collective_id=0, has_side_effects=True, vmem_limit_bytes=44 * 1024 * 1024
        ),
        name="spread",
    )(*(pltpu.with_memory_space_constraint(a, pltpu.HBM) for a in (traces, table, partner, block_ids)))


def correlate_kernel(scale, lhs, rem, out):
    k, r = pl.program_id(0), pl.program_id(1)
    chunks, n_win = rem.shape[:2]
    channels = lhs.shape[2]
    chans = channels // CCH
    parts_v = chunks // chans
    columns = []
    for h in range(chans):
        rows = [
            rem[h * parts_v + v, :, r, 2 * k + c].reshape(n_win * WCH, CCH)
            for c in range(2)
            for v in range(parts_v)
        ]
        columns.append(jnp.concatenate(rows, axis=0))
    right = jnp.concatenate(columns, axis=1)
    for t in range(2):
        out[0, 0, t] = jnp.dot(lhs[k, t], right, preferred_element_type=jnp.float32) * scale


def correlate(lhs, rem, scale):
    bins, _, channels, _ = lhs.shape
    out_shape = (ROUNDS, bins, 2, channels, channels)
    return pl.pallas_call(
        functools.partial(correlate_kernel, scale),
        grid=(bins, ROUNDS),
        out_shape=jax.ShapeDtypeStruct(out_shape, jnp.float32),
        in_specs=[pl.BlockSpec(memory_space=pltpu.VMEM)] * 2,
        out_specs=pl.BlockSpec((1, 1, 2, channels, channels), lambda k, r: (r, k, 0, 0, 0)),
        compiler_params=pltpu.CompilerParams(vmem_limit_bytes=16 * 1024 * 1024),
        name="correlate",
    )(lhs, rem)


def local(traces, partner, block_ids):
    windows = traces.shape[1] * N_WIN
    lhs, rem = spread(traces, partner, block_ids)
    return correlate(lhs, rem, 1.0 / math.sqrt(windows))


def solution(mesh):
    placed = (P("pair", "win", None), P(), P())
    return jax.shard_map(
        local,
        mesh=mesh,
        in_specs=placed,
        out_specs=P(None, "win", None, "pair", None),
        check_vma=False,
    )
```

```python
import functools
import math

import jax
import jax.numpy as jnp
import numpy as np
from jax import lax
from jax.experimental import pallas as pl
from jax.experimental.pallas import tpu as pltpu
from jax.sharding import PartitionSpec as P

SAMPLES = 1024
BINS = 32
FIRST_BIN = 16
BIN_STEP = 8
ROUNDS = 2
NY = 4
NZ = 4
N_WIN = 2 * NZ
N_COL = NY * 2
BINS_DEV = BINS // N_WIN
COL_STEPS = ((2, 0), (1, 0), (3, 0), (2, 1), (1, 1), (3, 1), (0, 1))
WIN_STEPS = ((1, 2), (1, 1), (1, 3), (0, 2), (1, 0), (0, 1), (0, 3))
PARTS = 2 * BINS_DEV
WCH = 8
AHEAD = 3
JOIN = 2
LAGS = (3, 6, 9)
CCH = 128
MESH = pl.DeviceIdType.MESH


def dft_columns():
    sample = np.arange(SAMPLES)
    freq = FIRST_BIN + BIN_STEP * np.arange(BINS)
    angle = 2.0 * np.pi / SAMPLES * (sample[:, None] * freq[None, :] % SAMPLES)
    taper = 0.5 - 0.5 * np.cos(2.0 * np.pi / SAMPLES * sample)
    both = np.stack([taper[:, None] * np.cos(angle), -taper[:, None] * np.sin(angle)], axis=2)
    return jnp.asarray(both.reshape(SAMPLES, 2 * BINS).astype(np.float32), dtype=jnp.bfloat16)


def spread_kernel(
    x_hbm, table_hbm, partner_hbm, ids_hbm, lhs_out, rem_out,
    table, partner, block_ids, raw0, raw1, ybuf, lhs, targets,
    xsem, tsem, s1, r1, s2, r2, s3, r3, s4, r4, l4, lsem, *buffers,
):
    pair = lax.axis_index("pair")
    win = lax.axis_index("win")
    xlo, col = pair // N_COL, pair % N_COL
    y, core = col // 2, col % 2
    xhi, z = win // NZ, win % NZ
    chunks = len(buffers) // 5
    xbufs, sends, owns, mids, sbufs = (buffers[i * chunks : (i + 1) * chunks] for i in range(5))
    raws = (raw0, raw1)
    parts_v = lhs.shape[3] // (2 * N_WIN * WCH)

    win_peers = [((xhi + a) % 2) * NZ + (z + b) % NZ for a, b in WIN_STEPS]
    col_peers = [((y + a) % NY) * 2 + (core + b) % 2 for a, b in COL_STEPS]
    mirror = ((1 - xlo) * N_COL + col, win)

    def x_copy(g):
        h, v = g // parts_v, g % parts_v
        return pltpu.make_async_copy(
            x_hbm.at[pl.ds(h * CCH, CCH), pl.ds(v * WCH, WCH)], xbufs[g], xsem.at[g]
        )

    table_copy = pltpu.make_async_copy(table_hbm, table, tsem.at[0])
    partner_copy = pltpu.make_async_copy(partner_hbm, partner, tsem.at[1])
    ids_copy = pltpu.make_async_copy(ids_hbm, block_ids, tsem.at[2])
    table_copy.start()
    for g in range(AHEAD):
        x_copy(g).start()
    partner_copy.start()
    ids_copy.start()

    barrier = pltpu.get_barrier_semaphore()
    for peer in win_peers:
        pl.semaphore_signal(barrier, inc=1, device_id=(pair, peer), device_id_type=MESH)
    for peer in col_peers:
        pl.semaphore_signal(barrier, inc=1, device_id=(xlo * N_COL + peer, win), device_id_type=MESH)
    pl.semaphore_signal(barrier, inc=1, device_id=mirror, device_id_type=MESH)

    def find_targets():
        partner_copy.wait()
        ids_copy.wait()

        @pl.loop(0, ROUNDS)
        def _(r):
            @pl.loop(0, N_COL)
            def _(d):
                wanted = partner[r, block_ids[xlo * N_COL + d]]
                found = jnp.int32(0)
                for q in range(2 * N_COL):
                    found = jnp.where(block_ids[q] == wanted, q, found)
                targets[r, d] = found

    def remote(src, dst, send, recv, device):
        return pltpu.make_async_remote_copy(
            src_ref=src, dst_ref=dst, send_sem=send, recv_sem=recv, device_id=device, device_id_type=MESH
        )

    blocks = 4
    rows = CCH * WCH // blocks

    def product(g, i):
        block = xbufs[g][pl.ds(i * (rows // WCH), rows // WCH)].reshape(rows, SAMPLES)
        raws[g % 2][pl.ds(i * rows, rows), :] = jnp.dot(block, table[...], preferred_element_type=jnp.float32)

    def whiten(g, w):
        part = raws[g % 2][pl.ds(w, CCH, stride=WCH), :].T[: 2 * BINS]
        power = jnp.sum(part * part, axis=0, keepdims=True) * (1.0 / (2 * BINS))
        ybuf[pl.ds(w, 2 * BINS, stride=WCH), :] = part * lax.rsqrt(power + 1e-05)

    def load(g):
        x_copy(g).wait()
        if g + AHEAD < chunks:
            x_copy(g + AHEAD).start()

    def product_all(g):
        load(g)

        @pl.loop(0, blocks)
        def _(i):
            product(g, i)

    def whiten_all(g):
        for w in range(WCH):
            whiten(g, w)

    def both(g):
        load(g + 1)

        @pl.loop(0, blocks)
        def _(i):
            product(g + 1, i)
            for w in range(WCH // blocks):
                whiten(g, i * (WCH // blocks) + w)

    def transform(g):
        if g == 0:
            table_copy.wait()
            product_all(0)
            whiten_all(0)
        elif g == chunks - 1:
            whiten_all(g)
        else:
            if g == 1:
                product_all(1)
            both(g)
        sends[g][...] = ybuf[...].astype(jnp.bfloat16).reshape(N_WIN, PARTS, WCH, CCH)

    def phase1(g):
        for peer in win_peers:
            remote(sends[g].at[peer], owns[g].at[win], s1.at[g], r1.at[g, win], (pair, peer)).start()
        owns[g][win] = sends[g][win]

    def phase2(g):
        for peer in win_peers:
            remote(sends[g].at[peer], owns[g].at[peer], s1.at[g], r1.at[g, peer], (pair, peer)).wait_recv()
        for peer in col_peers:
            remote(
                owns[g].at[peer], mids[g].at[pair], s2.at[g], r2.at[g, col], (xlo * N_COL + peer, win)
            ).start()
        mids[g][pair] = owns[g][col]

    def phase3(g):
        remote(mids[g].at[pair], mids[g].at[pair], s3.at[g], r3.at[g], mirror).start()
        for peer in col_peers:
            slot = xlo * N_COL + peer
            remote(owns[g].at[peer], mids[g].at[slot], s2.at[g], r2.at[g, peer], (slot, win)).wait_recv()
            remote(mids[g].at[slot], mids[g].at[slot], s3.at[g], r3.at[g], mirror).start()

    def phase4(g):
        theirs = mids[g].at[pl.ds((1 - xlo) * N_COL, N_COL)]
        remote(theirs, theirs, s3.at[g], r3.at[g], mirror).wait_recv()
        for peer in [*col_peers, col]:
            for r in range(ROUNDS):
                sbufs[g][peer, r] = mids[g][targets[r, peer]]
            if peer is col:
                pltpu.make_async_copy(sbufs[g].at[col], rem_out.at[g, col], l4.at[g]).start()
            else:
                remote(
                    sbufs[g].at[peer], rem_out.at[g, col], s4.at[g], r4.at[g], (xlo * N_COL + peer, win)
                ).start()

    def left_side(g):
        h, v = g // parts_v, g % parts_v
        to = pl.ds(h * CCH, CCH)
        span = N_WIN * WCH
        for k in range(BINS_DEV):
            for c in range(2):
                part = jnp.concatenate(
                    [owns[g + j][:, 2 * k + c].reshape(span, CCH).astype(jnp.float32) for j in range(JOIN)], axis=0
                ).T
                plain = part.astype(jnp.bfloat16)
                turned = (part if c else -part).astype(jnp.bfloat16)
                lhs[k, 0, to, pl.ds((c * parts_v + v) * span, JOIN * span)] = plain
                lhs[k, 1, to, pl.ds(((1 - c) * parts_v + v) * span, JOIN * span)] = turned

    lag2, lag3, lag4 = LAGS
    lhs_copy = pltpu.make_async_copy(lhs, lhs_out, lsem)
    for t in range(chunks + lag4):
        if t < chunks:
            transform(t)
            if t == 0:
                pl.semaphore_wait(barrier, len(win_peers) + len(col_peers) + 1)
            phase1(t)
            if t == 0:
                find_targets()
        if 0 <= t - lag2 < chunks:
            phase2(t - lag2)
        if 0 <= t - lag3 < chunks:
            phase3(t - lag3)
        g = t - lag3 - JOIN + 1
        if 0 <= g < chunks and g % JOIN == 0:
            left_side(g)
            if g == chunks - JOIN:
                lhs_copy.start()
        if 0 <= t - lag4 < chunks:
            phase4(t - lag4)

    lhs_copy.wait()
    for g in range(chunks):
        seven = owns[g].at[pl.ds(0, N_WIN - 1)]
        eight = mids[g].at[pl.ds(0, N_COL)]
        rounds = sbufs[g].at[pl.ds(0, N_COL - 1)]
        landed = rem_out.at[g, pl.ds(0, N_COL - 1)]
        remote(seven, seven, s1.at[g], r1.at[g, 0], mirror).wait_send()
        remote(seven, seven, s2.at[g], r2.at[g, 0], mirror).wait_send()
        remote(eight, eight, s3.at[g], r3.at[g], mirror).wait_send()
        remote(rounds, landed, s4.at[g], r4.at[g], mirror).wait_send()
        pltpu.make_async_copy(sbufs[g].at[col], rem_out.at[g, col], l4.at[g]).wait()
        remote(rounds, landed, s4.at[g], r4.at[g], mirror).wait_recv()


def spread(traces, partner, block_ids):
    channels, windows, _ = traces.shape
    chunks = (channels // CCH) * (windows // WCH)
    piece = (PARTS, WCH, CCH)
    bf16, f32 = jnp.bfloat16, jnp.float32
    lhs_shape = (BINS_DEV, 2, channels, 2 * N_WIN * windows)
    rem_shape = (chunks, N_COL, ROUNDS, *piece)
    dma = pltpu.SemaphoreType.DMA
    table = jnp.pad(dft_columns(), ((0, 0), (0, 128 - 2 * BINS)))
    return pl.pallas_call(
        spread_kernel,
        out_shape=(jax.ShapeDtypeStruct(lhs_shape, bf16), jax.ShapeDtypeStruct(rem_shape, bf16)),
        in_specs=[pl.BlockSpec(memory_space=pltpu.HBM)] * 4,
        out_specs=(pl.BlockSpec(memory_space=pl.ANY), pl.BlockSpec(memory_space=pl.ANY)),
        scratch_shapes=[
            pltpu.VMEM(table.shape, bf16),
            pltpu.SMEM(partner.shape, jnp.int32),
            pltpu.SMEM(block_ids.shape, jnp.int32),
            pltpu.VMEM((CCH * WCH, 128), f32),
            pltpu.VMEM((CCH * WCH, 128), f32),
            pltpu.VMEM((2 * BINS * WCH, CCH), f32),
            pltpu.VMEM(lhs_shape, bf16),
            pltpu.SMEM((ROUNDS, N_COL), jnp.int32),
            dma((chunks,)), dma((3,)),
            dma((chunks,)), dma((chunks, N_WIN)),
            dma((chunks,)), dma((chunks, N_COL)),
            dma((chunks,)), dma((chunks,)),
            dma((chunks,)), dma((chunks,)),
            dma((chunks,)),
            dma,
            *[pltpu.VMEM((CCH, WCH, SAMPLES), bf16)] * chunks,
            *[pltpu.VMEM((N_WIN, *piece), bf16)] * (2 * chunks),
            *[pltpu.VMEM((2 * N_COL, *piece), bf16)] * chunks,
            *[pltpu.VMEM((N_COL, ROUNDS, *piece), bf16)] * chunks,
        ],
        compiler_params=pltpu.CompilerParams(
            collective_id=0, has_side_effects=True, vmem_limit_bytes=44 * 1024 * 1024
        ),
        name="spread",
    )(*(pltpu.with_memory_space_constraint(a, pltpu.HBM) for a in (traces, table, partner, block_ids)))


def correlate_kernel(scale, lhs, rem, out_hbm, out, sems):
    chunks, n_win = rem.shape[:2]
    bins, _, channels, _ = lhs.shape
    chans = channels // CCH
    parts_v = chunks // chans
    copies = []
    for k in range(bins):
        for r in range(ROUNDS):
            columns = []
            for h in range(chans):
                rows = [
                    rem[h * parts_v + v, :, r, 2 * k + c].reshape(n_win * WCH, CCH)
                    for c in range(2)
                    for v in range(parts_v)
                ]
                columns.append(jnp.concatenate(rows, axis=0))
            right = jnp.concatenate(columns, axis=1)
            for t in range(2):
                out[r, k, t] = jnp.dot(lhs[k, t], right, preferred_element_type=jnp.float32) * scale
            copies.append(pltpu.make_async_copy(out.at[r, k], out_hbm.at[r, k], sems.at[len(copies)]))
            copies[-1].start()
    for copy in copies:
        copy.wait()


def correlate(lhs, rem, scale):
    bins, _, channels, _ = lhs.shape
    out_shape = (ROUNDS, bins, 2, channels, channels)
    return pl.pallas_call(
        functools.partial(correlate_kernel, scale),
        out_shape=jax.ShapeDtypeStruct(out_shape, jnp.float32),
        in_specs=[pl.BlockSpec(memory_space=pltpu.VMEM)] * 2,
        out_specs=pl.BlockSpec(memory_space=pltpu.HBM),
        scratch_shapes=[pltpu.VMEM(out_shape, jnp.float32), pltpu.SemaphoreType.DMA((bins * ROUNDS,))],
        compiler_params=pltpu.CompilerParams(vmem_limit_bytes=16 * 1024 * 1024),
        name="correlate",
    )(lhs, rem)


def local(traces, partner, block_ids):
    windows = traces.shape[1] * N_WIN
    lhs, rem = spread(traces, partner, block_ids)
    return correlate(lhs, rem, 1.0 / math.sqrt(windows))


def solution(mesh):
    placed = (P("pair", "win", None), P(), P())
    return jax.shard_map(
        local,
        mesh=mesh,
        in_specs=placed,
        out_specs=P(None, "win", None, "pair", None),
        check_vma=False,
    )
```

```python
import functools
import math

import jax
import jax.numpy as jnp
import numpy as np
from jax import lax
from jax.experimental import pallas as pl
from jax.experimental.pallas import tpu as pltpu
from jax.sharding import PartitionSpec as P

SAMPLES = 1024
BINS = 32
FIRST_BIN = 16
BIN_STEP = 8
ROUNDS = 2
NY = 4
NZ = 4
N_WIN = 2 * NZ
N_COL = NY * 2
BINS_DEV = BINS // N_WIN
COL_STEPS = ((2, 0), (1, 0), (3, 0), (2, 1), (1, 1), (3, 1), (0, 1))
WIN_STEPS = ((1, 2), (1, 1), (1, 3), (0, 2), (1, 0), (0, 1), (0, 3))
PARTS = 2 * BINS_DEV
WCH = 8
AHEAD = 3
JOIN = 2
LAGS = (3, 6, 9)
CCH = 128
MESH = pl.DeviceIdType.MESH


def dft_columns():
    sample = np.arange(SAMPLES)
    freq = FIRST_BIN + BIN_STEP * np.arange(BINS)
    angle = 2.0 * np.pi / SAMPLES * (sample[:, None] * freq[None, :] % SAMPLES)
    taper = 0.5 - 0.5 * np.cos(2.0 * np.pi / SAMPLES * sample)
    both = np.stack([taper[:, None] * np.cos(angle), -taper[:, None] * np.sin(angle)], axis=2)
    return jnp.asarray(both.reshape(SAMPLES, 2 * BINS).astype(np.float32), dtype=jnp.bfloat16)


def spread_kernel(
    x_hbm, table_hbm, partner_hbm, ids_hbm, lhs_out, rem_out,
    table, partner, block_ids, raw0, raw1, ybuf, lhs, targets,
    xsem, fsem, tsem, s1, r1, s2, r2, s3, r3, s4, r4, l4, lsem, *buffers,
):
    pair = lax.axis_index("pair")
    win = lax.axis_index("win")
    xlo, col = pair // N_COL, pair % N_COL
    y, core = col // 2, col % 2
    xhi, z = win // NZ, win % NZ
    chunks = len(buffers) // 5
    xbufs, sends, owns, mids, sbufs = (buffers[i * chunks : (i + 1) * chunks] for i in range(5))
    raws = (raw0, raw1)
    parts_v = lhs.shape[3] // (2 * N_WIN * WCH)

    win_peers = [((xhi + a) % 2) * NZ + (z + b) % NZ for a, b in WIN_STEPS]
    col_peers = [((y + a) % NY) * 2 + (core + b) % 2 for a, b in COL_STEPS]
    mirror = ((1 - xlo) * N_COL + col, win)

    def x_copy(g):
        h, v = g // parts_v, g % parts_v
        return pltpu.make_async_copy(
            x_hbm.at[pl.ds(h * CCH, CCH), pl.ds(v * WCH, WCH)], xbufs[g], xsem.at[g]
        )

    blocks = fsem.shape[0]
    rows = CCH * WCH // blocks

    def first_copy(i):
        span = CCH // blocks
        return pltpu.make_async_copy(
            x_hbm.at[pl.ds(i * span, span), pl.ds(0, WCH)], xbufs[0].at[pl.ds(i * span, span)], fsem.at[i]
        )

    table_copy = pltpu.make_async_copy(table_hbm, table, tsem.at[0])
    partner_copy = pltpu.make_async_copy(partner_hbm, partner, tsem.at[1])
    ids_copy = pltpu.make_async_copy(ids_hbm, block_ids, tsem.at[2])
    for i in range(blocks):
        first_copy(i).start()
        if i == 0:
            table_copy.start()
    for g in range(1, AHEAD):
        x_copy(g).start()
    partner_copy.start()
    ids_copy.start()

    barrier = pltpu.get_barrier_semaphore()
    for peer in win_peers:
        pl.semaphore_signal(barrier, inc=1, device_id=(pair, peer), device_id_type=MESH)
    for peer in col_peers:
        pl.semaphore_signal(barrier, inc=1, device_id=(xlo * N_COL + peer, win), device_id_type=MESH)
    pl.semaphore_signal(barrier, inc=1, device_id=mirror, device_id_type=MESH)

    def find_targets():
        partner_copy.wait()
        ids_copy.wait()

        @pl.loop(0, ROUNDS)
        def _(r):
            @pl.loop(0, N_COL)
            def _(d):
                wanted = partner[r, block_ids[xlo * N_COL + d]]
                found = jnp.int32(0)
                for q in range(2 * N_COL):
                    found = jnp.where(block_ids[q] == wanted, q, found)
                targets[r, d] = found

    def remote(src, dst, send, recv, device):
        return pltpu.make_async_remote_copy(
            src_ref=src, dst_ref=dst, send_sem=send, recv_sem=recv, device_id=device, device_id_type=MESH
        )

    def product(g, i):
        block = xbufs[g][pl.ds(i * (rows // WCH), rows // WCH)].reshape(rows, SAMPLES)
        raws[g % 2][pl.ds(i * rows, rows), :] = jnp.dot(block, table[...], preferred_element_type=jnp.float32)

    def whiten(g, w):
        part = raws[g % 2][pl.ds(w, CCH, stride=WCH), :].T[: 2 * BINS]
        power = jnp.sum(part * part, axis=0, keepdims=True) * (1.0 / (2 * BINS))
        ybuf[pl.ds(w, 2 * BINS, stride=WCH), :] = part * lax.rsqrt(power + 1e-05)

    def load(g):
        x_copy(g).wait()
        if g + AHEAD - 1 < chunks:
            x_copy(g + AHEAD - 1).start()

    def product_first():
        table_copy.wait()
        for i in range(blocks):
            first_copy(i).wait()
            product(0, i)

    def whiten_all(g):
        for w in range(WCH):
            whiten(g, w)

    def both(g):
        load(g + 1)

        @pl.loop(0, blocks)
        def _(i):
            product(g + 1, i)
            for w in range(WCH // blocks):
                whiten(g, i * (WCH // blocks) + w)

    def transform(g):
        if g == 0:
            product_first()
        if g < chunks - 1:
            both(g)
        else:
            whiten_all(g)
        sends[g][...] = ybuf[...].astype(jnp.bfloat16).reshape(N_WIN, PARTS, WCH, CCH)

    def phase1(g):
        for peer in win_peers:
            remote(sends[g].at[peer], owns[g].at[win], s1.at[g], r1.at[g, win], (pair, peer)).start()
        owns[g][win] = sends[g][win]

    def phase2(g):
        for peer in win_peers:
            remote(sends[g].at[peer], owns[g].at[peer], s1.at[g], r1.at[g, peer], (pair, peer)).wait_recv()
        for peer in col_peers:
            remote(
                owns[g].at[peer], mids[g].at[pair], s2.at[g], r2.at[g, col], (xlo * N_COL + peer, win)
            ).start()
        mids[g][pair] = owns[g][col]

    def phase3(g):
        remote(mids[g].at[pair], mids[g].at[pair], s3.at[g], r3.at[g], mirror).start()
        for peer in col_peers:
            slot = xlo * N_COL + peer
            remote(owns[g].at[peer], mids[g].at[slot], s2.at[g], r2.at[g, peer], (slot, win)).wait_recv()
            remote(mids[g].at[slot], mids[g].at[slot], s3.at[g], r3.at[g], mirror).start()

    def phase4(g):
        theirs = mids[g].at[pl.ds((1 - xlo) * N_COL, N_COL)]
        remote(theirs, theirs, s3.at[g], r3.at[g], mirror).wait_recv()
        for peer in [*col_peers, col]:
            for r in range(ROUNDS):
                sbufs[g][peer, r] = mids[g][targets[r, peer]]
            if peer is col:
                pltpu.make_async_copy(sbufs[g].at[col], rem_out.at[g, col], l4.at[g]).start()
            else:
                remote(
                    sbufs[g].at[peer], rem_out.at[g, col], s4.at[g], r4.at[g], (xlo * N_COL + peer, win)
                ).start()

    def left_side(g):
        h, v = g // parts_v, g % parts_v
        to = pl.ds(h * CCH, CCH)
        span = N_WIN * WCH
        for k in range(BINS_DEV):
            for c in range(2):
                part = jnp.concatenate(
                    [owns[g + j][:, 2 * k + c].reshape(span, CCH).astype(jnp.float32) for j in range(JOIN)], axis=0
                ).T
                plain = part.astype(jnp.bfloat16)
                turned = (part if c else -part).astype(jnp.bfloat16)
                lhs[k, 0, to, pl.ds((c * parts_v + v) * span, JOIN * span)] = plain
                lhs[k, 1, to, pl.ds(((1 - c) * parts_v + v) * span, JOIN * span)] = turned

    lag2, lag3, lag4 = LAGS
    lhs_copy = pltpu.make_async_copy(lhs, lhs_out, lsem)
    for t in range(chunks + lag4):
        if t < chunks:
            transform(t)
            if t == 0:
                pl.semaphore_wait(barrier, len(win_peers) + len(col_peers) + 1)
            phase1(t)
        if t == lag3:
            find_targets()
        if 0 <= t - lag2 < chunks:
            phase2(t - lag2)
        if 0 <= t - lag3 < chunks:
            phase3(t - lag3)
        g = t - lag3 - JOIN + 1
        if 0 <= g < chunks and g % JOIN == 0:
            left_side(g)
            if g == chunks - JOIN:
                lhs_copy.start()
        if 0 <= t - lag4 < chunks:
            phase4(t - lag4)

    lhs_copy.wait()
    for g in range(chunks):
        seven = owns[g].at[pl.ds(0, N_WIN - 1)]
        eight = mids[g].at[pl.ds(0, N_COL)]
        rounds = sbufs[g].at[pl.ds(0, N_COL - 1)]
        landed = rem_out.at[g, pl.ds(0, N_COL - 1)]
        remote(seven, seven, s1.at[g], r1.at[g, 0], mirror).wait_send()
        remote(seven, seven, s2.at[g], r2.at[g, 0], mirror).wait_send()
        remote(eight, eight, s3.at[g], r3.at[g], mirror).wait_send()
        remote(rounds, landed, s4.at[g], r4.at[g], mirror).wait_send()
        pltpu.make_async_copy(sbufs[g].at[col], rem_out.at[g, col], l4.at[g]).wait()
        remote(rounds, landed, s4.at[g], r4.at[g], mirror).wait_recv()


def spread(traces, partner, block_ids):
    channels, windows, _ = traces.shape
    chunks = (channels // CCH) * (windows // WCH)
    piece = (PARTS, WCH, CCH)
    bf16, f32 = jnp.bfloat16, jnp.float32
    lhs_shape = (BINS_DEV, 2, channels, 2 * N_WIN * windows)
    rem_shape = (chunks, N_COL, ROUNDS, *piece)
    dma = pltpu.SemaphoreType.DMA
    table = jnp.pad(dft_columns(), ((0, 0), (0, 128 - 2 * BINS)))
    return pl.pallas_call(
        spread_kernel,
        out_shape=(jax.ShapeDtypeStruct(lhs_shape, bf16), jax.ShapeDtypeStruct(rem_shape, bf16)),
        in_specs=[pl.BlockSpec(memory_space=pltpu.HBM)] * 4,
        out_specs=(pl.BlockSpec(memory_space=pl.ANY), pl.BlockSpec(memory_space=pl.ANY)),
        scratch_shapes=[
            pltpu.VMEM(table.shape, bf16),
            pltpu.SMEM(partner.shape, jnp.int32),
            pltpu.SMEM(block_ids.shape, jnp.int32),
            pltpu.VMEM((CCH * WCH, 128), f32),
            pltpu.VMEM((CCH * WCH, 128), f32),
            pltpu.VMEM((2 * BINS * WCH, CCH), f32),
            pltpu.VMEM(lhs_shape, bf16),
            pltpu.SMEM((ROUNDS, N_COL), jnp.int32),
            dma((chunks,)), dma((4,)), dma((3,)),
            dma((chunks,)), dma((chunks, N_WIN)),
            dma((chunks,)), dma((chunks, N_COL)),
            dma((chunks,)), dma((chunks,)),
            dma((chunks,)), dma((chunks,)),
            dma((chunks,)),
            dma,
            *[pltpu.VMEM((CCH, WCH, SAMPLES), bf16)] * chunks,
            *[pltpu.VMEM((N_WIN, *piece), bf16)] * (2 * chunks),
            *[pltpu.VMEM((2 * N_COL, *piece), bf16)] * chunks,
            *[pltpu.VMEM((N_COL, ROUNDS, *piece), bf16)] * chunks,
        ],
        compiler_params=pltpu.CompilerParams(
            collective_id=0, has_side_effects=True, vmem_limit_bytes=44 * 1024 * 1024
        ),
        name="spread",
    )(*(pltpu.with_memory_space_constraint(a, pltpu.HBM) for a in (traces, table, partner, block_ids)))


def correlate_kernel(scale, lhs, rem, out_hbm, out, sems):
    chunks, n_win = rem.shape[:2]
    bins, _, channels, _ = lhs.shape
    chans = channels // CCH
    parts_v = chunks // chans
    copies = []
    for k in range(bins):
        for r in range(ROUNDS):
            columns = []
            for h in range(chans):
                rows = [
                    rem[h * parts_v + v, :, r, 2 * k + c].reshape(n_win * WCH, CCH)
                    for c in range(2)
                    for v in range(parts_v)
                ]
                columns.append(jnp.concatenate(rows, axis=0))
            right = jnp.concatenate(columns, axis=1)
            for t in range(2):
                out[r, k, t] = jnp.dot(lhs[k, t], right, preferred_element_type=jnp.float32) * scale
            copies.append(pltpu.make_async_copy(out.at[r, k], out_hbm.at[r, k], sems.at[len(copies)]))
            copies[-1].start()
    for copy in copies:
        copy.wait()


def correlate(lhs, rem, scale):
    bins, _, channels, _ = lhs.shape
    out_shape = (ROUNDS, bins, 2, channels, channels)
    return pl.pallas_call(
        functools.partial(correlate_kernel, scale),
        out_shape=jax.ShapeDtypeStruct(out_shape, jnp.float32),
        in_specs=[pl.BlockSpec(memory_space=pltpu.VMEM)] * 2,
        out_specs=pl.BlockSpec(memory_space=pltpu.HBM),
        scratch_shapes=[pltpu.VMEM(out_shape, jnp.float32), pltpu.SemaphoreType.DMA((bins * ROUNDS,))],
        compiler_params=pltpu.CompilerParams(vmem_limit_bytes=16 * 1024 * 1024),
        name="correlate",
    )(lhs, rem)


def local(traces, partner, block_ids):
    windows = traces.shape[1] * N_WIN
    lhs, rem = spread(traces, partner, block_ids)
    return correlate(lhs, rem, 1.0 / math.sqrt(windows))


def solution(mesh):
    placed = (P("pair", "win", None), P(), P())
    return jax.shard_map(
        local,
        mesh=mesh,
        in_specs=placed,
        out_specs=P(None, "win", None, "pair", None),
        check_vma=False,
    )
```

```python
import functools
import math

import jax
import jax.numpy as jnp
import numpy as np
from jax import lax
from jax.experimental import pallas as pl
from jax.experimental.pallas import tpu as pltpu
from jax.sharding import PartitionSpec as P

SAMPLES = 1024
BINS = 32
FIRST_BIN = 16
BIN_STEP = 8
ROUNDS = 2
NY = 4
NZ = 4
N_WIN = 2 * NZ
N_COL = NY * 2
BINS_DEV = BINS // N_WIN
COL_STEPS = ((2, 0), (1, 0), (3, 0), (2, 1), (1, 1), (3, 1), (0, 1))
WIN_STEPS = ((1, 2), (1, 1), (1, 3), (0, 2), (1, 0), (0, 1), (0, 3))
PARTS = 2 * BINS_DEV
WCH = 8
AHEAD = 3
JOIN = 2
LAGS = (3, 7, 10)
CCH = 128
MESH = pl.DeviceIdType.MESH


def dft_columns():
    sample = np.arange(SAMPLES)
    freq = FIRST_BIN + BIN_STEP * np.arange(BINS)
    angle = 2.0 * np.pi / SAMPLES * (sample[:, None] * freq[None, :] % SAMPLES)
    taper = 0.5 - 0.5 * np.cos(2.0 * np.pi / SAMPLES * sample)
    both = np.stack([taper[:, None] * np.cos(angle), -taper[:, None] * np.sin(angle)], axis=2)
    return jnp.asarray(both.reshape(SAMPLES, 2 * BINS).astype(np.float32), dtype=jnp.bfloat16)


def spread_kernel(
    x_hbm, table_hbm, partner_hbm, ids_hbm, lhs_out, rem_out,
    table, partner, block_ids, raw0, raw1, ybuf, lhs, targets,
    xsem, fsem, tsem, s1, r1, s2, r2, s3, r3, s4, r4, l4, lsem, *buffers,
):
    pair = lax.axis_index("pair")
    win = lax.axis_index("win")
    xlo, col = pair // N_COL, pair % N_COL
    y, core = col // 2, col % 2
    xhi, z = win // NZ, win % NZ
    chunks = len(buffers) // 5
    xbufs, sends, owns, mids, sbufs = (buffers[i * chunks : (i + 1) * chunks] for i in range(5))
    raws = (raw0, raw1)
    parts_v = lhs.shape[3] // (2 * N_WIN * WCH)

    win_peers = [((xhi + a) % 2) * NZ + (z + b) % NZ for a, b in WIN_STEPS]
    col_peers = [((y + a) % NY) * 2 + (core + b) % 2 for a, b in COL_STEPS]
    mirror = ((1 - xlo) * N_COL + col, win)

    def x_copy(g):
        h, v = g // parts_v, g % parts_v
        return pltpu.make_async_copy(
            x_hbm.at[pl.ds(h * CCH, CCH), pl.ds(v * WCH, WCH)], xbufs[g], xsem.at[g]
        )

    blocks = fsem.shape[0]
    rows = CCH * WCH // blocks

    def first_copy(i):
        span = CCH // blocks
        return pltpu.make_async_copy(
            x_hbm.at[pl.ds(i * span, span), pl.ds(0, WCH)], xbufs[0].at[pl.ds(i * span, span)], fsem.at[i]
        )

    table_copy = pltpu.make_async_copy(table_hbm, table, tsem.at[0])
    partner_copy = pltpu.make_async_copy(partner_hbm, partner, tsem.at[1])
    ids_copy = pltpu.make_async_copy(ids_hbm, block_ids, tsem.at[2])
    for i in range(blocks):
        first_copy(i).start()
        if i == 0:
            table_copy.start()
    for g in range(1, AHEAD):
        x_copy(g).start()
    partner_copy.start()
    ids_copy.start()

    barrier = pltpu.get_barrier_semaphore()
    for peer in win_peers:
        pl.semaphore_signal(barrier, inc=1, device_id=(pair, peer), device_id_type=MESH)
    for peer in col_peers:
        pl.semaphore_signal(barrier, inc=1, device_id=(xlo * N_COL + peer, win), device_id_type=MESH)
    pl.semaphore_signal(barrier, inc=1, device_id=mirror, device_id_type=MESH)

    def find_targets():
        partner_copy.wait()
        ids_copy.wait()

        @pl.loop(0, ROUNDS)
        def _(r):
            @pl.loop(0, N_COL)
            def _(d):
                wanted = partner[r, block_ids[xlo * N_COL + d]]
                found = jnp.int32(0)
                for q in range(2 * N_COL):
                    found = jnp.where(block_ids[q] == wanted, q, found)
                targets[r, d] = found

    def remote(src, dst, send, recv, device):
        return pltpu.make_async_remote_copy(
            src_ref=src, dst_ref=dst, send_sem=send, recv_sem=recv, device_id=device, device_id_type=MESH
        )

    def product(g, i):
        block = xbufs[g][pl.ds(i * (rows // WCH), rows // WCH)].reshape(rows, SAMPLES)
        raws[g % 2][pl.ds(i * rows, rows), :] = jnp.dot(block, table[...], preferred_element_type=jnp.float32)

    def whiten(g, w):
        part = raws[g % 2][pl.ds(w, CCH, stride=WCH), :].T[: 2 * BINS]
        power = jnp.sum(part * part, axis=0, keepdims=True) * (1.0 / (2 * BINS))
        ybuf[pl.ds(w, 2 * BINS, stride=WCH), :] = part * lax.rsqrt(power + 1e-05)

    def load(g):
        x_copy(g).wait()
        if g + AHEAD - 1 < chunks:
            x_copy(g + AHEAD - 1).start()

    def product_first():
        table_copy.wait()
        for i in range(blocks):
            first_copy(i).wait()
            product(0, i)

    def whiten_all(g):
        for w in range(WCH):
            whiten(g, w)

    def both(g):
        load(g + 1)

        @pl.loop(0, blocks)
        def _(i):
            product(g + 1, i)
            for w in range(WCH // blocks):
                whiten(g, i * (WCH // blocks) + w)

    def transform(g):
        if g == 0:
            product_first()
        if g < chunks - 1:
            both(g)
        else:
            whiten_all(g)
        sends[g][...] = ybuf[...].astype(jnp.bfloat16).reshape(N_WIN, PARTS, WCH, CCH)

    def phase1(g):
        for peer in win_peers:
            remote(sends[g].at[peer], owns[g].at[win], s1.at[g], r1.at[g, win], (pair, peer)).start()
        owns[g][win] = sends[g][win]

    def phase2(g):
        def forward(part):
            @pl.when(part != col)
            def _():
                device = (xlo * N_COL + part, win)
                remote(owns[g].at[part], mids[g].at[pair], s2.at[g], r2.at[g, col], device).start()

            @pl.when(part == col)
            def _():
                mids[g][pair] = owns[g][part]

        forward(win)
        for peer in reversed(win_peers):
            remote(sends[g].at[peer], owns[g].at[peer], s1.at[g], r1.at[g, peer], (pair, peer)).wait_recv()
            forward(peer)

    def phase3(g):
        remote(mids[g].at[pair], mids[g].at[pair], s3.at[g], r3.at[g], mirror).start()
        for peer in col_peers:
            slot = xlo * N_COL + peer
            remote(owns[g].at[peer], mids[g].at[slot], s2.at[g], r2.at[g, peer], (slot, win)).wait_recv()
            remote(mids[g].at[slot], mids[g].at[slot], s3.at[g], r3.at[g], mirror).start()

    def phase4(g):
        theirs = mids[g].at[pl.ds((1 - xlo) * N_COL, N_COL)]
        remote(theirs, theirs, s3.at[g], r3.at[g], mirror).wait_recv()
        for peer in [*col_peers, col]:
            for r in range(ROUNDS):
                sbufs[g][peer, r] = mids[g][targets[r, peer]]
            if peer is col:
                pltpu.make_async_copy(sbufs[g].at[col], rem_out.at[g, col], l4.at[g]).start()
            else:
                remote(
                    sbufs[g].at[peer], rem_out.at[g, col], s4.at[g], r4.at[g], (xlo * N_COL + peer, win)
                ).start()

    def left_side(g):
        h, v = g // parts_v, g % parts_v
        to = pl.ds(h * CCH, CCH)
        span = N_WIN * WCH
        for k in range(BINS_DEV):
            for c in range(2):
                part = jnp.concatenate(
                    [owns[g + j][:, 2 * k + c].reshape(span, CCH).astype(jnp.float32) for j in range(JOIN)], axis=0
                ).T
                plain = part.astype(jnp.bfloat16)
                turned = (part if c else -part).astype(jnp.bfloat16)
                lhs[k, 0, to, pl.ds((c * parts_v + v) * span, JOIN * span)] = plain
                lhs[k, 1, to, pl.ds(((1 - c) * parts_v + v) * span, JOIN * span)] = turned

    lag2, lag3, lag4 = LAGS
    lhs_copy = pltpu.make_async_copy(lhs, lhs_out, lsem)
    for t in range(chunks + lag4):
        if t < chunks:
            transform(t)
            if t == 0:
                pl.semaphore_wait(barrier, len(win_peers) + len(col_peers) + 1)
            phase1(t)
        if t == lag3:
            find_targets()
        if 0 <= t - lag2 < chunks:
            phase2(t - lag2)
        if 0 <= t - lag3 < chunks:
            phase3(t - lag3)
        g = t - lag3 - JOIN + 1
        if 0 <= g < chunks and g % JOIN == 0:
            left_side(g)
            if g == chunks - JOIN:
                lhs_copy.start()
        if 0 <= t - lag4 < chunks:
            phase4(t - lag4)

    lhs_copy.wait()
    for g in range(chunks):
        seven = owns[g].at[pl.ds(0, N_WIN - 1)]
        eight = mids[g].at[pl.ds(0, N_COL)]
        rounds = sbufs[g].at[pl.ds(0, N_COL - 1)]
        landed = rem_out.at[g, pl.ds(0, N_COL - 1)]
        remote(seven, seven, s1.at[g], r1.at[g, 0], mirror).wait_send()
        remote(seven, seven, s2.at[g], r2.at[g, 0], mirror).wait_send()
        remote(eight, eight, s3.at[g], r3.at[g], mirror).wait_send()
        remote(rounds, landed, s4.at[g], r4.at[g], mirror).wait_send()
        pltpu.make_async_copy(sbufs[g].at[col], rem_out.at[g, col], l4.at[g]).wait()
        remote(rounds, landed, s4.at[g], r4.at[g], mirror).wait_recv()


def spread(traces, partner, block_ids):
    channels, windows, _ = traces.shape
    chunks = (channels // CCH) * (windows // WCH)
    piece = (PARTS, WCH, CCH)
    bf16, f32 = jnp.bfloat16, jnp.float32
    lhs_shape = (BINS_DEV, 2, channels, 2 * N_WIN * windows)
    rem_shape = (chunks, N_COL, ROUNDS, *piece)
    dma = pltpu.SemaphoreType.DMA
    table = jnp.pad(dft_columns(), ((0, 0), (0, 128 - 2 * BINS)))
    return pl.pallas_call(
        spread_kernel,
        out_shape=(jax.ShapeDtypeStruct(lhs_shape, bf16), jax.ShapeDtypeStruct(rem_shape, bf16)),
        in_specs=[pl.BlockSpec(memory_space=pltpu.HBM)] * 4,
        out_specs=(pl.BlockSpec(memory_space=pl.ANY), pl.BlockSpec(memory_space=pl.ANY)),
        scratch_shapes=[
            pltpu.VMEM(table.shape, bf16),
            pltpu.SMEM(partner.shape, jnp.int32),
            pltpu.SMEM(block_ids.shape, jnp.int32),
            pltpu.VMEM((CCH * WCH, 128), f32),
            pltpu.VMEM((CCH * WCH, 128), f32),
            pltpu.VMEM((2 * BINS * WCH, CCH), f32),
            pltpu.VMEM(lhs_shape, bf16),
            pltpu.SMEM((ROUNDS, N_COL), jnp.int32),
            dma((chunks,)), dma((4,)), dma((3,)),
            dma((chunks,)), dma((chunks, N_WIN)),
            dma((chunks,)), dma((chunks, N_COL)),
            dma((chunks,)), dma((chunks,)),
            dma((chunks,)), dma((chunks,)),
            dma((chunks,)),
            dma,
            *[pltpu.VMEM((CCH, WCH, SAMPLES), bf16)] * chunks,
            *[pltpu.VMEM((N_WIN, *piece), bf16)] * (2 * chunks),
            *[pltpu.VMEM((2 * N_COL, *piece), bf16)] * chunks,
            *[pltpu.VMEM((N_COL, ROUNDS, *piece), bf16)] * chunks,
        ],
        compiler_params=pltpu.CompilerParams(
            collective_id=0, has_side_effects=True, vmem_limit_bytes=44 * 1024 * 1024
        ),
        name="spread",
    )(*(pltpu.with_memory_space_constraint(a, pltpu.HBM) for a in (traces, table, partner, block_ids)))


def correlate_kernel(scale, lhs, rem, out_hbm, out, sems):
    chunks, n_win = rem.shape[:2]
    bins, _, channels, _ = lhs.shape
    chans = channels // CCH
    parts_v = chunks // chans
    copies = []
    for k in range(bins):
        for r in range(ROUNDS):
            columns = []
            for h in range(chans):
                rows = [
                    rem[h * parts_v + v, :, r, 2 * k + c].reshape(n_win * WCH, CCH)
                    for c in range(2)
                    for v in range(parts_v)
                ]
                columns.append(jnp.concatenate(rows, axis=0))
            right = jnp.concatenate(columns, axis=1)
            for t in range(2):
                out[r, k, t] = jnp.dot(lhs[k, t], right, preferred_element_type=jnp.float32) * scale
            copies.append(pltpu.make_async_copy(out.at[r, k], out_hbm.at[r, k], sems.at[len(copies)]))
            copies[-1].start()
    for copy in copies:
        copy.wait()


def correlate(lhs, rem, scale):
    bins, _, channels, _ = lhs.shape
    out_shape = (ROUNDS, bins, 2, channels, channels)
    return pl.pallas_call(
        functools.partial(correlate_kernel, scale),
        out_shape=jax.ShapeDtypeStruct(out_shape, jnp.float32),
        in_specs=[pl.BlockSpec(memory_space=pltpu.VMEM)] * 2,
        out_specs=pl.BlockSpec(memory_space=pltpu.HBM),
        scratch_shapes=[pltpu.VMEM(out_shape, jnp.float32), pltpu.SemaphoreType.DMA((bins * ROUNDS,))],
        compiler_params=pltpu.CompilerParams(vmem_limit_bytes=16 * 1024 * 1024),
        name="correlate",
    )(lhs, rem)


def local(traces, partner, block_ids):
    windows = traces.shape[1] * N_WIN
    lhs, rem = spread(traces, partner, block_ids)
    return correlate(lhs, rem, 1.0 / math.sqrt(windows))


def solution(mesh):
    placed = (P("pair", "win", None), P(), P())
    return jax.shard_map(
        local,
        mesh=mesh,
        in_specs=placed,
        out_specs=P(None, "win", None, "pair", None),
        check_vma=False,
    )
```

```python
import functools
import math

import jax
import jax.numpy as jnp
import numpy as np
from jax import lax
from jax.experimental import pallas as pl
from jax.experimental.pallas import tpu as pltpu
from jax.sharding import PartitionSpec as P

SAMPLES = 1024
BINS = 32
FIRST_BIN = 16
BIN_STEP = 8
ROUNDS = 2
NY = 4
NZ = 4
N_WIN = 2 * NZ
N_COL = NY * 2
BINS_DEV = BINS // N_WIN
COL_STEPS = ((2, 0), (1, 0), (3, 0), (2, 1), (1, 1), (3, 1), (0, 1))
WIN_STEPS = ((1, 2), (1, 1), (1, 3), (0, 2), (1, 0), (0, 1), (0, 3))
PARTS = 2 * BINS_DEV
WCH = 8
AHEAD = 3
JOIN = 2
LAGS = (4, 7, 11)
CCH = 128
MESH = pl.DeviceIdType.MESH


def dft_columns():
    sample = np.arange(SAMPLES)
    freq = FIRST_BIN + BIN_STEP * np.arange(BINS)
    angle = 2.0 * np.pi / SAMPLES * (sample[:, None] * freq[None, :] % SAMPLES)
    taper = 0.5 - 0.5 * np.cos(2.0 * np.pi / SAMPLES * sample)
    both = np.stack([taper[:, None] * np.cos(angle), -taper[:, None] * np.sin(angle)], axis=2)
    return jnp.asarray(both.reshape(SAMPLES, 2 * BINS).astype(np.float32), dtype=jnp.bfloat16)


def spread_kernel(
    x_hbm, table_hbm, partner_hbm, ids_hbm, lhs_out, rem_out,
    table, partner, block_ids, raw0, raw1, ybuf, lhs, targets,
    xsem, fsem, tsem, s1, r1, s2, r2, s3, r3, s4, r4, l4, lsem, *buffers,
):
    pair = lax.axis_index("pair")
    win = lax.axis_index("win")
    xlo, col = pair // N_COL, pair % N_COL
    y, core = col // 2, col % 2
    xhi, z = win // NZ, win % NZ
    chunks = len(buffers) // 5
    xbufs, sends, owns, mids, sbufs = (buffers[i * chunks : (i + 1) * chunks] for i in range(5))
    raws = (raw0, raw1)
    parts_v = lhs.shape[3] // (2 * N_WIN * WCH)

    win_peers = [((xhi + a) % 2) * NZ + (z + b) % NZ for a, b in WIN_STEPS]
    col_peers = [((y + a) % NY) * 2 + (core + b) % 2 for a, b in COL_STEPS]
    mirror = ((1 - xlo) * N_COL + col, win)

    def x_copy(g):
        h, v = g // parts_v, g % parts_v
        return pltpu.make_async_copy(
            x_hbm.at[pl.ds(h * CCH, CCH), pl.ds(v * WCH, WCH)], xbufs[g], xsem.at[g]
        )

    blocks = fsem.shape[0]
    rows = CCH * WCH // blocks

    def first_copy(i):
        span = CCH // blocks
        return pltpu.make_async_copy(
            x_hbm.at[pl.ds(i * span, span), pl.ds(0, WCH)], xbufs[0].at[pl.ds(i * span, span)], fsem.at[i]
        )

    table_copy = pltpu.make_async_copy(table_hbm, table, tsem.at[0])
    partner_copy = pltpu.make_async_copy(partner_hbm, partner, tsem.at[1])
    ids_copy = pltpu.make_async_copy(ids_hbm, block_ids, tsem.at[2])
    for i in range(blocks):
        first_copy(i).start()
        if i == 0:
            table_copy.start()
    for g in range(1, AHEAD):
        x_copy(g).start()
    partner_copy.start()
    ids_copy.start()

    barrier = pltpu.get_barrier_semaphore()
    for peer in win_peers:
        pl.semaphore_signal(barrier, inc=1, device_id=(pair, peer), device_id_type=MESH)
    for peer in col_peers:
        pl.semaphore_signal(barrier, inc=1, device_id=(xlo * N_COL + peer, win), device_id_type=MESH)
    pl.semaphore_signal(barrier, inc=1, device_id=mirror, device_id_type=MESH)

    def find_targets():
        partner_copy.wait()
        ids_copy.wait()

        @pl.loop(0, ROUNDS)
        def _(r):
            @pl.loop(0, N_COL)
            def _(d):
                wanted = partner[r, block_ids[xlo * N_COL + d]]
                found = jnp.int32(0)
                for q in range(2 * N_COL):
                    found = jnp.where(block_ids[q] == wanted, q, found)
                targets[r, d] = found

    def remote(src, dst, send, recv, device):
        return pltpu.make_async_remote_copy(
            src_ref=src, dst_ref=dst, send_sem=send, recv_sem=recv, device_id=device, device_id_type=MESH
        )

    def product(g, i):
        block = xbufs[g][pl.ds(i * (rows // WCH), rows // WCH)].reshape(rows, SAMPLES)
        raws[g % 2][pl.ds(i * rows, rows), :] = jnp.dot(block, table[...], preferred_element_type=jnp.float32)

    def whiten(g, w):
        part = raws[g % 2][pl.ds(w, CCH, stride=WCH), :].T[: 2 * BINS]
        power = jnp.sum(part * part, axis=0, keepdims=True) * (1.0 / (2 * BINS))
        ybuf[pl.ds(w, 2 * BINS, stride=WCH), :] = part * lax.rsqrt(power + 1e-05)

    def load(g):
        x_copy(g).wait()
        if g + AHEAD - 1 < chunks:
            x_copy(g + AHEAD - 1).start()

    def product_first():
        table_copy.wait()
        for i in range(blocks):
            first_copy(i).wait()
            product(0, i)

    def whiten_all(g):
        for w in range(WCH):
            whiten(g, w)

    def both(g):
        load(g + 1)

        @pl.loop(0, blocks)
        def _(i):
            product(g + 1, i)
            for w in range(WCH // blocks):
                whiten(g, i * (WCH // blocks) + w)

    def transform(g):
        if g == 0:
            product_first()
        if g < chunks - 1:
            both(g)
        else:
            whiten_all(g)
        sends[g][...] = ybuf[...].astype(jnp.bfloat16).reshape(N_WIN, PARTS, WCH, CCH)

    def phase1(g):
        for peer in win_peers:
            remote(sends[g].at[peer], owns[g].at[win], s1.at[g], r1.at[g, win], (pair, peer)).start()
        owns[g][win] = sends[g][win]

    def phase2(g):
        def forward(part):
            @pl.when(part != col)
            def _():
                device = (xlo * N_COL + part, win)
                remote(owns[g].at[part], mids[g].at[pair], s2.at[g], r2.at[g, col], device).start()

            @pl.when(part == col)
            def _():
                mids[g][pair] = owns[g][part]

        forward(win)
        for peer in reversed(win_peers):
            remote(sends[g].at[peer], owns[g].at[peer], s1.at[g], r1.at[g, peer], (pair, peer)).wait_recv()
            forward(peer)

    def phase3(g):
        remote(mids[g].at[pair], mids[g].at[pair], s3.at[g], r3.at[g], mirror).start()
        for peer in col_peers:
            slot = xlo * N_COL + peer
            remote(owns[g].at[peer], mids[g].at[slot], s2.at[g], r2.at[g, peer], (slot, win)).wait_recv()
            remote(mids[g].at[slot], mids[g].at[slot], s3.at[g], r3.at[g], mirror).start()

    def phase4(g):
        theirs = mids[g].at[pl.ds((1 - xlo) * N_COL, N_COL)]
        remote(theirs, theirs, s3.at[g], r3.at[g], mirror).wait_recv()
        for peer in [*col_peers, col]:
            for r in range(ROUNDS):
                sbufs[g][peer, r] = mids[g][targets[r, peer]]
            if peer is col:
                pltpu.make_async_copy(sbufs[g].at[col], rem_out.at[g, col], l4.at[g]).start()
            else:
                remote(
                    sbufs[g].at[peer], rem_out.at[g, col], s4.at[g], r4.at[g], (xlo * N_COL + peer, win)
                ).start()

    def left_side(g):
        h, v = g // parts_v, g % parts_v
        to = pl.ds(h * CCH, CCH)
        span = N_WIN * WCH
        for k in range(BINS_DEV):
            for c in range(2):
                part = jnp.concatenate(
                    [owns[g + j][:, 2 * k + c].reshape(span, CCH).astype(jnp.float32) for j in range(JOIN)], axis=0
                ).T
                plain = part.astype(jnp.bfloat16)
                turned = (part if c else -part).astype(jnp.bfloat16)
                lhs[k, 0, to, pl.ds((c * parts_v + v) * span, JOIN * span)] = plain
                lhs[k, 1, to, pl.ds(((1 - c) * parts_v + v) * span, JOIN * span)] = turned

    lag2, lag3, lag4 = LAGS
    lhs_copy = pltpu.make_async_copy(lhs, lhs_out, lsem)
    for t in range(chunks + lag4):
        if t < chunks:
            transform(t)
            if t == 0:
                pl.semaphore_wait(barrier, len(win_peers) + len(col_peers) + 1)
            phase1(t)
        if t == lag3:
            find_targets()
        if 0 <= t - lag2 < chunks:
            phase2(t - lag2)
        if 0 <= t - lag3 < chunks:
            phase3(t - lag3)
        g = t - lag3 - JOIN + 1
        if 0 <= g < chunks and g % JOIN == 0:
            left_side(g)
            if g == chunks - JOIN:
                lhs_copy.start()
        if 0 <= t - lag4 < chunks:
            phase4(t - lag4)

    lhs_copy.wait()
    for g in range(chunks):
        seven = owns[g].at[pl.ds(0, N_WIN - 1)]
        eight = mids[g].at[pl.ds(0, N_COL)]
        rounds = sbufs[g].at[pl.ds(0, N_COL - 1)]
        landed = rem_out.at[g, pl.ds(0, N_COL - 1)]
        remote(seven, seven, s1.at[g], r1.at[g, 0], mirror).wait_send()
        remote(seven, seven, s2.at[g], r2.at[g, 0], mirror).wait_send()
        remote(eight, eight, s3.at[g], r3.at[g], mirror).wait_send()
        remote(rounds, landed, s4.at[g], r4.at[g], mirror).wait_send()
        pltpu.make_async_copy(sbufs[g].at[col], rem_out.at[g, col], l4.at[g]).wait()
        remote(rounds, landed, s4.at[g], r4.at[g], mirror).wait_recv()


def spread(traces, partner, block_ids):
    channels, windows, _ = traces.shape
    chunks = (channels // CCH) * (windows // WCH)
    piece = (PARTS, WCH, CCH)
    bf16, f32 = jnp.bfloat16, jnp.float32
    lhs_shape = (BINS_DEV, 2, channels, 2 * N_WIN * windows)
    rem_shape = (chunks, N_COL, ROUNDS, *piece)
    dma = pltpu.SemaphoreType.DMA
    table = jnp.pad(dft_columns(), ((0, 0), (0, 128 - 2 * BINS)))
    return pl.pallas_call(
        spread_kernel,
        out_shape=(jax.ShapeDtypeStruct(lhs_shape, bf16), jax.ShapeDtypeStruct(rem_shape, bf16)),
        in_specs=[pl.BlockSpec(memory_space=pltpu.HBM)] * 4,
        out_specs=(pl.BlockSpec(memory_space=pl.ANY), pl.BlockSpec(memory_space=pl.ANY)),
        scratch_shapes=[
            pltpu.VMEM(table.shape, bf16),
            pltpu.SMEM(partner.shape, jnp.int32),
            pltpu.SMEM(block_ids.shape, jnp.int32),
            pltpu.VMEM((CCH * WCH, 128), f32),
            pltpu.VMEM((CCH * WCH, 128), f32),
            pltpu.VMEM((2 * BINS * WCH, CCH), f32),
            pltpu.VMEM(lhs_shape, bf16),
            pltpu.SMEM((ROUNDS, N_COL), jnp.int32),
            dma((chunks,)), dma((4,)), dma((3,)),
            dma((chunks,)), dma((chunks, N_WIN)),
            dma((chunks,)), dma((chunks, N_COL)),
            dma((chunks,)), dma((chunks,)),
            dma((chunks,)), dma((chunks,)),
            dma((chunks,)),
            dma,
            *[pltpu.VMEM((CCH, WCH, SAMPLES), bf16)] * chunks,
            *[pltpu.VMEM((N_WIN, *piece), bf16)] * (2 * chunks),
            *[pltpu.VMEM((2 * N_COL, *piece), bf16)] * chunks,
            *[pltpu.VMEM((N_COL, ROUNDS, *piece), bf16)] * chunks,
        ],
        compiler_params=pltpu.CompilerParams(
            collective_id=0, has_side_effects=True, vmem_limit_bytes=44 * 1024 * 1024
        ),
        name="spread",
    )(*(pltpu.with_memory_space_constraint(a, pltpu.HBM) for a in (traces, table, partner, block_ids)))


def correlate_kernel(scale, lhs, rem, out_hbm, out, sems):
    chunks, n_win = rem.shape[:2]
    bins, _, channels, _ = lhs.shape
    chans = channels // CCH
    parts_v = chunks // chans
    copies = []
    for k in range(bins):
        for r in range(ROUNDS):
            columns = []
            for h in range(chans):
                rows = [
                    rem[h * parts_v + v, :, r, 2 * k + c].reshape(n_win * WCH, CCH)
                    for c in range(2)
                    for v in range(parts_v)
                ]
                columns.append(jnp.concatenate(rows, axis=0))
            right = jnp.concatenate(columns, axis=1)
            for t in range(2):
                out[r, k, t] = jnp.dot(lhs[k, t], right, preferred_element_type=jnp.float32) * scale
            copies.append(pltpu.make_async_copy(out.at[r, k], out_hbm.at[r, k], sems.at[len(copies)]))
            copies[-1].start()
    for copy in copies:
        copy.wait()


def correlate(lhs, rem, scale):
    bins, _, channels, _ = lhs.shape
    out_shape = (ROUNDS, bins, 2, channels, channels)
    return pl.pallas_call(
        functools.partial(correlate_kernel, scale),
        out_shape=jax.ShapeDtypeStruct(out_shape, jnp.float32),
        in_specs=[pl.BlockSpec(memory_space=pltpu.VMEM)] * 2,
        out_specs=pl.BlockSpec(memory_space=pltpu.HBM),
        scratch_shapes=[pltpu.VMEM(out_shape, jnp.float32), pltpu.SemaphoreType.DMA((bins * ROUNDS,))],
        compiler_params=pltpu.CompilerParams(vmem_limit_bytes=16 * 1024 * 1024),
        name="correlate",
    )(lhs, rem)


def local(traces, partner, block_ids):
    windows = traces.shape[1] * N_WIN
    lhs, rem = spread(traces, partner, block_ids)
    return correlate(lhs, rem, 1.0 / math.sqrt(windows))


def solution(mesh):
    placed = (P("pair", "win", None), P(), P())
    return jax.shard_map(
        local,
        mesh=mesh,
        in_specs=placed,
        out_specs=P(None, "win", None, "pair", None),
        check_vma=False,
    )
```
